32 devices in a mesh: row: 8 (over z, y), col: 4 (over x, core).
Axes of the slice: x: 2, y: 2, z: 4, core: 2. Of those that a mesh axis runs over, the one named last changes fastest.
Arguments:
- rhs_grid: float32 [65536, 512], P(('row', 'col')), may hold values from -6 to 6
- leaf_order: int32 [128, 512], P(('row', 'col')), may hold values from 0 to 511, each once within a row
- source_basis: float32 [128, 512, 192], P(('row', 'col')), may hold values from -0.25 to 0.25
- transfer: float32 [7, 128, 192, 384], P(None, ('row', 'col')), may hold values from -0.3125 to 0.3125
- target_basis: float32 [128, 512, 192], P(('row', 'col')), may hold values from -0.4375 to 0.4375
Outputs:
- result: float32 [65536, 512], P(('row', 'col'))
The draws below stay inside these ranges and needn't reach their ends.
Inputs may be any that keep to these rules, and one draw needn't show every extreme that they name: Each row of leaf_order names every one of 0 to 511 once.
All inputs are finite; a program needn't handle non-finite values.
Results may differ from the reference program's by a relative error of at most 0.00013.
Values sent between devices are 32-bit elements; how exact they have to be, the bound alone decides.
A program may use at most 128 MiB of HBM per device.

```python
import jax
import jax.numpy as jnp
from jax import lax

LEAF = 512
RANK = 192
RHS = 512
LOCAL_BITS = 2
ROW_BITS = 3
COL_BITS = 2
LEVELS = 7
LEAVES = 128
NPTS = 65536


def block_scale(key, dims, pieces, least, largest):
    def one(axis_at, shards_of):
        heights = jax.random.uniform(jax.random.fold_in(jax.random.fold_in(key, 6), axis_at), (shards_of,), jnp.float32, least / len(pieces), largest / len(pieces))
        return jnp.repeat(jnp.exp(heights), dims[axis_at] // shards_of).reshape((-1,) + (1,) * (len(dims) - axis_at - 1))

    gain = one(*pieces[0])
    for cut in pieces[1:]:
        gain = gain * one(*cut)
    return gain


def gaussian(key, dims, deviation, reach, cuts=(), dtype=jnp.bfloat16):
    values = deviation * jax.random.normal(key, dims, jnp.float32)
    if cuts:
        values = values * block_scale(key, dims, cuts, -0.22, 0.18)
    return jnp.clip(values, -reach, reach).astype(dtype)


def setup_inputs(seed: int = 0) -> dict:
    key_of = jax.random.split(jax.random.key(seed), 6)
    return {
        "rhs_grid": gaussian(key_of[0], (NPTS, RHS), 1.0, 6.0, ((0, 32),), jnp.float32),
        "leaf_order": jax.vmap(lambda own: jax.random.permutation(own, LEAF))(jax.random.split(key_of[1], LEAVES)).reshape((LEAVES, LEAF)).astype(jnp.int32),
        "source_basis": gaussian(key_of[2], (LEAVES, LEAF, RANK), LEAF ** -0.5, 0.25, ((0, 32),), jnp.float32),
        "transfer": gaussian(key_of[3], (LEVELS, LEAVES, RANK, 2 * RANK), (2 * RANK) ** -0.5, 0.3125, ((1, 32),), jnp.float32),
        "target_basis": gaussian(key_of[4], (LEAVES, LEAF, RANK), RANK ** -0.5, 0.4375, ((0, 32),), jnp.float32),
    }


PRECISE = lax.Precision.HIGHEST


def partner_of(values, bit_pos):
    node_count = values.shape[0]
    halves = values.reshape((node_count // (2 ** (bit_pos + 1)), 2, 2 ** bit_pos) + values.shape[1:])
    return halves[:, ::-1].reshape(values.shape)


def place_rows(basis, order):
    def single(leaf_block, leaf_index):
        return jnp.zeros_like(leaf_block).at[leaf_index].set(leaf_block)
    return jax.vmap(single)(basis, order)


def reference(rhs_grid, leaf_order, source_basis, transfer, target_basis):
    bit_order = list(range(LOCAL_BITS)) + [LOCAL_BITS + COL_BITS + offset for offset in range(ROW_BITS)] + [LOCAL_BITS + offset for offset in range(COL_BITS)]
    placed_in = place_rows(source_basis, leaf_order)
    current = jnp.einsum("lqk,lqr->lkr", placed_in, rhs_grid.reshape(LEAVES, LEAF, RHS), precision=PRECISE)
    for section in range(LEVELS):
        blocks = transfer[section]
        other = partner_of(current, bit_order[section])
        own_term = jnp.einsum("nij,njr->nir", blocks[:, :, :RANK], current, precision=PRECISE)
        current = own_term + jnp.einsum("nij,njr->nir", blocks[:, :, RANK:], other, precision=PRECISE)
    placed_out = place_rows(target_basis, leaf_order)
    result = jnp.einsum("lqk,lkr->lqr", placed_out, current, precision=PRECISE)
    return result.reshape(NPTS, RHS)
```

```python
import functools

import jax
import jax.numpy as jnp
from jax import lax
from jax.experimental import pallas as pl
from jax.experimental.pallas import tpu as pltpu
from jax.sharding import PartitionSpec as P

F32 = jnp.float32
BF16 = jnp.bfloat16
WIDTH = 128


def split(value):
    high = value.astype(BF16)
    return high, (value - high.astype(F32)).astype(BF16)


def dot(a, b):
    return jnp.dot(a, b, preferred_element_type=F32)


def dot3(a_parts, b_parts):
    (a_high, a_low), (b_high, b_low) = a_parts, b_parts
    return dot(a_high, b_high) + (dot(a_high, b_low) + dot(a_low, b_high))


def partner_id(axis, bit_pos):
    mask = 2**bit_pos
    here = lax.axis_index(axis)
    return {axis: here + mask * (1 - 2 * ((here // mask) % 2))}


def kernel(
    stages, offsets, low_bits,
    rhs, order, source, transfer, target, out,
    rhs_v, source_v, target_v, transfer_v, in_high, in_low, out_high, out_low,
    sent, received, staged, rhs_sem, load_sem, transfer_sem, send_sem, recv_sem, out_sem,
):
    leaf_count, leaf_rows = order.shape
    chunks = rhs_v.shape[0]
    units = leaf_count * chunks

    load_source = pltpu.make_async_copy(source, source_v, load_sem.at[0])
    load_target = pltpu.make_async_copy(target, target_v, load_sem.at[1])

    def load_rhs(chunk):
        return pltpu.make_async_copy(
            rhs.at[:, pl.ds(pl.multiple_of(chunk * WIDTH, WIDTH), WIDTH)], rhs_v.at[chunk], rhs_sem.at[chunk]
        )

    def load_transfer(level):
        return pltpu.make_async_copy(transfer.at[level], transfer_v.at[level], transfer_sem.at[level])

    levels = transfer.shape[0]
    load_source.start()
    load_rhs(0).start()
    for level in range(low_bits):
        load_transfer(level).start()
    for level in range(low_bits, levels):
        load_transfer(level).start()
    for chunk in range(1, chunks):
        load_rhs(chunk).start()
    load_target.start()

    barrier = pltpu.get_barrier_semaphore()
    for stage in stages:
        pl.semaphore_signal(barrier, inc=1, device_id=partner_id(*stage), device_id_type=pl.DeviceIdType.MESH)

    def selection(leaf):
        grid_row = lax.broadcasted_iota(jnp.int32, (leaf_rows, leaf_rows), 0)
        named = jnp.broadcast_to(order[pl.ds(leaf, 1), :], (leaf_rows, leaf_rows))
        return jnp.where(grid_row == named, 1.0, 0.0).astype(BF16)

    def place_in(leaf):
        chosen = selection(leaf)
        for part, kept in zip(split(source_v[leaf].T), (in_high, in_low)):
            kept[leaf] = lax.dot_general(
                part, chosen, (((1,), (1,)), ((), ())), preferred_element_type=F32
            ).astype(BF16)

    def place_out(leaf):
        chosen = selection(leaf)
        for part, kept in zip(split(target_v[leaf]), (out_high, out_low)):
            kept[leaf] = dot(chosen, part).astype(BF16)

    def exchange(stage, unit):
        return pltpu.make_async_remote_copy(
            src_ref=sent.at[stage, unit],
            dst_ref=received.at[stage, unit],
            send_sem=send_sem.at[stage, unit],
            recv_sem=recv_sem.at[stage, unit],
            device_id=partner_id(*stages[stage]),
            device_id_type=pl.DeviceIdType.MESH,
        )

    def write_out(unit):
        leaf, chunk = unit % leaf_count, unit // leaf_count
        return pltpu.make_async_copy(
            staged.at[unit],
            out.at[
                pl.ds(pl.multiple_of(leaf * leaf_rows, leaf_rows), leaf_rows),
                pl.ds(pl.multiple_of(chunk * WIDTH, WIDTH), WIDTH),
            ],
            out_sem.at[unit],
        )

    def combine(level, node, own, other):
        return dot3(split(transfer_v[level, node]), split(jnp.concatenate([own, other], axis=0)))

    def enter(chunk):
        load_rhs(chunk).wait()
        current = []
        for leaf in range(leaf_count):
            rows = rhs_v[chunk, pl.ds(leaf * leaf_rows, leaf_rows), :]
            current.append(dot3((in_high[leaf], in_low[leaf]), split(rows)))
        for level in range(low_bits):
            current = [
                combine(level, node, current[node], current[node ^ 2**level]) for node in range(leaf_count)
            ]
        for node in range(leaf_count):
            unit = chunk * leaf_count + node
            sent[0, unit] = current[node]
            exchange(0, unit).start()

    def advance(stage, unit):
        node = unit % leaf_count
        exchange(stage, unit).wait_recv()
        value = combine(low_bits + stage, node, sent[stage, unit], received[stage, unit])
        if stage + 1 < len(stages):
            sent[stage + 1, unit] = value
            exchange(stage + 1, unit).start()
        else:
            staged[unit] = dot3((out_high[node], out_low[node]), split(value))
            write_out(unit).start()

    load_source.wait()
    for leaf in range(leaf_count):
        place_in(leaf)
    for level in range(low_bits):
        load_transfer(level).wait()
    pl.semaphore_wait(barrier, len(stages))
    enter(0)
    for level in range(low_bits, levels):
        load_transfer(level).wait()
    load_target.wait()

    @pl.loop(0, units + offsets[-1])
    def _(tick):
        for stage in range(len(stages)):
            unit = tick - offsets[stage]

            @pl.when((unit >= 0) & (unit < units))
            def _():
                advance(stage, unit)

        @pl.when(tick < leaf_count)
        def _():
            place_out(tick)

        @pl.when((tick % leaf_count == 1) & (tick // leaf_count + 1 < chunks))
        def _():
            enter(tick // leaf_count + 1)

    @pl.loop(0, units)
    def _(unit):
        for stage in range(len(stages)):
            exchange(stage, unit).wait_send()
        write_out(unit).wait()


def on_device(rhs_grid, leaf_order, source_basis, transfer, target_basis):
    leaf_count, leaf_rows = leaf_order.shape
    points, columns = rhs_grid.shape
    rank = source_basis.shape[2]
    levels = transfer.shape[0]
    low_bits = leaf_count.bit_length() - 1
    row_bits = lax.axis_size("row").bit_length() - 1
    col_bits = lax.axis_size("col").bit_length() - 1
    stages = [("row", bit) for bit in range(row_bits)] + [("col", bit) for bit in range(col_bits)]
    count = len(stages)
    offsets = [stage for stage in range(count)]
    offsets[-1] = max(offsets[-1], leaf_count)
    chunks = columns // WIDTH
    units = leaf_count * chunks
    hbm = pl.BlockSpec(memory_space=pl.ANY)
    return pl.pallas_call(
        functools.partial(kernel, stages, offsets, low_bits),
        out_shape=jax.ShapeDtypeStruct((points, columns), F32),
        in_specs=[hbm, pl.BlockSpec(memory_space=pltpu.VMEM), hbm, hbm, hbm],
        out_specs=hbm,
        scratch_shapes=[
            pltpu.VMEM((chunks, points, WIDTH), F32),
            pltpu.VMEM(source_basis.shape, F32),
            pltpu.VMEM(target_basis.shape, F32),
            pltpu.VMEM(transfer.shape, F32),
            pltpu.VMEM((leaf_count, rank, leaf_rows), BF16),
            pltpu.VMEM((leaf_count, rank, leaf_rows), BF16),
            pltpu.VMEM((leaf_count, leaf_rows, rank), BF16),
            pltpu.VMEM((leaf_count, leaf_rows, rank), BF16),
            pltpu.VMEM((count, units, rank, WIDTH), F32),
            pltpu.VMEM((count, units, rank, WIDTH), F32),
            pltpu.VMEM((units, leaf_rows, WIDTH), F32),
            pltpu.SemaphoreType.DMA((chunks,)),
            pltpu.SemaphoreType.DMA((2,)),
            pltpu.SemaphoreType.DMA((levels,)),
            pltpu.SemaphoreType.DMA((count, units)),
            pltpu.SemaphoreType.DMA((count, units)),
            pltpu.SemaphoreType.DMA((units,)),
        ],
        compiler_params=pltpu.CompilerParams(
            collective_id=0, has_side_effects=True, vmem_limit_bytes=60 * 2**20
        ),
    )(rhs_grid, leaf_order, source_basis, transfer, target_basis)


def solution(mesh):
    in_specs = (
        P(("row", "col"), None),
        P(("row", "col"), None),
        P(("row", "col"), None, None),
        P(None, ("row", "col"), None, None),
        P(("row", "col"), None, None),
    )
    out_specs = P(("row", "col"), None)
    return jax.shard_map(
        on_device, mesh=mesh, in_specs=in_specs, out_specs=out_specs, check_vma=False
    )
```

```python
import functools

import jax
import jax.numpy as jnp
from jax import lax
from jax.experimental import pallas as pl
from jax.experimental.pallas import tpu as pltpu
from jax.sharding import PartitionSpec as P

F32 = jnp.float32
BF16 = jnp.bfloat16
WIDTH = 128
MIDDLE = 2
FAR = 3
PLACE_AT = 6


def split(value):
    high = value.astype(BF16)
    return high, (value - high.astype(F32)).astype(BF16)


def dot(a, b):
    return jnp.dot(a, b, preferred_element_type=F32)


def dot3(a_parts, b_parts):
    (a_high, a_low), (b_high, b_low) = a_parts, b_parts
    width = b_high.shape[1]
    both = dot(a_high, jnp.concatenate([b_high, b_low], axis=1))
    return both[:, :width] + (both[:, width:] + dot(a_low, b_high))


def partner_id(axis, bit_pos):
    mask = 2**bit_pos
    here = lax.axis_index(axis)
    return {axis: here + mask * (1 - 2 * ((here // mask) % 2))}


def kernel(
    stages, offsets, low_bits,
    rhs, order, source, transfer, target, out, placed,
    rhs_v, source_v, target_v, transfer_v, in_high, in_low, placed_v,
    sent, received, staged, rhs_sem, load_sem, transfer_sem, send_sem, recv_sem, out_sem, placed_sem,
):
    leaf_count, leaf_rows = order.shape
    chunks = rhs_v.shape[0]
    units = leaf_count * chunks

    load_target = pltpu.make_async_copy(target, target_v, load_sem.at[leaf_count])

    def load_source(leaf):
        return pltpu.make_async_copy(source.at[leaf], source_v.at[leaf], load_sem.at[leaf])

    def load_rhs(chunk):
        return pltpu.make_async_copy(
            rhs.at[:, pl.ds(pl.multiple_of(chunk * WIDTH, WIDTH), WIDTH)], rhs_v.at[chunk], rhs_sem.at[chunk]
        )

    def load_transfer(level):
        return pltpu.make_async_copy(transfer.at[level], transfer_v.at[level], transfer_sem.at[level])

    levels = transfer.shape[0]
    for leaf in range(leaf_count):
        load_source(leaf).start()
    load_rhs(0).start()
    for level in range(low_bits + 2):
        load_transfer(level).start()
    load_rhs(1).start()
    for level in range(low_bits + 2, levels):
        load_transfer(level).start()
    for chunk in range(2, chunks):
        load_rhs(chunk).start()
    load_target.start()

    barrier = pltpu.get_barrier_semaphore()
    for stage in stages:
        pl.semaphore_signal(barrier, inc=1, device_id=partner_id(*stage), device_id_type=pl.DeviceIdType.MESH)

    def selection(leaf):
        grid_row = lax.broadcasted_iota(jnp.int32, (leaf_rows, leaf_rows), 0)
        named = jnp.broadcast_to(order[pl.ds(leaf, 1), :], (leaf_rows, leaf_rows))
        return jnp.where(grid_row == named, 1.0, 0.0).astype(BF16)

    def place_in(leaf):
        parts = jnp.concatenate(split(source_v[leaf]), axis=0)
        rows = lax.dot_general(
            parts, selection(leaf), (((1,), (1,)), ((), ())), preferred_element_type=F32
        ).astype(BF16)
        in_high[leaf] = rows[: source_v.shape[1]]
        in_low[leaf] = rows[source_v.shape[1] :]

    def place_out(leaf):
        chosen = selection(leaf)
        for index, part in enumerate(split(target_v[leaf])):
            placed_v[leaf, index] = lax.dot_general(
                chosen, part, (((1,), (1,)), ((), ())), preferred_element_type=F32
            ).astype(BF16)
        write_placed(leaf).start()

    def write_placed(leaf):
        return pltpu.make_async_copy(placed_v.at[leaf], placed.at[leaf], placed_sem.at[leaf])

    def exchange(stage, unit):
        return pltpu.make_async_remote_copy(
            src_ref=sent.at[stage, unit],
            dst_ref=received.at[stage, unit],
            send_sem=send_sem.at[stage, unit],
            recv_sem=recv_sem.at[stage, unit],
            device_id=partner_id(*stages[stage]),
            device_id_type=pl.DeviceIdType.MESH,
        )

    def write_out(unit):
        leaf, chunk = unit % leaf_count, unit // leaf_count
        return pltpu.make_async_copy(
            staged.at[unit],
            out.at[leaf, :, :, pl.ds(pl.multiple_of(chunk * WIDTH, WIDTH), WIDTH)],
            out_sem.at[unit],
        )

    def combine(level, node, own, other):
        return dot3(split(transfer_v[level, node]), split(jnp.concatenate([own, other], axis=0)))

    def enter(chunk):
        load_rhs(chunk).wait()
        current = []
        for leaf in range(leaf_count):
            rows = rhs_v[chunk, pl.ds(leaf * leaf_rows, leaf_rows), :]
            current.append(dot3((in_high[leaf], in_low[leaf]), split(rows)))
        for level in range(low_bits - 1):
            current = [
                combine(level, node, current[node], current[node ^ 2**level]) for node in range(leaf_count)
            ]
        last = low_bits - 1
        for node in range(leaf_count):
            unit = chunk * leaf_count + node
            if low_bits:
                sent[0, unit] = combine(last, node, current[node], current[node ^ 2**last])
            else:
                sent[0, unit] = current[node]
            exchange(0, unit).start()

    def advance(stage, unit):
        node = unit % leaf_count
        exchange(stage, unit).wait_recv()
        value = combine(low_bits + stage, node, sent[stage, unit], received[stage, unit])
        if stage + 1 < len(stages):
            sent[stage + 1, unit] = value
            exchange(stage + 1, unit).start()
        else:
            for index, part in enumerate(split(value)):
                staged[unit, index] = part
            write_out(unit).start()

    for leaf in range(leaf_count):
        load_source(leaf).wait()
        place_in(leaf)
    for level in range(low_bits):
        load_transfer(level).wait()
    pl.semaphore_wait(barrier, len(stages))
    enter(0)

    near = [stage for stage in range(len(stages)) if stages[stage] == ("col", 0)]
    turns = near + [stage for stage in reversed(range(len(stages))) if stage not in near]

    @pl.loop(0, units + offsets[-1])
    def _(tick):
        for stage in turns:
            unit = tick - offsets[stage]

            @pl.when(unit == 0)
            def _():
                load_transfer(low_bits + stage).wait()

            @pl.when((unit >= 0) & (unit < units))
            def _():
                advance(stage, unit)

        @pl.when(tick == PLACE_AT - 1)
        def _():
            load_target.wait()

        @pl.when((tick >= PLACE_AT) & (tick < PLACE_AT + leaf_count))
        def _():
            place_out(tick - PLACE_AT)

        @pl.when((tick % leaf_count == 1) & (tick // leaf_count + 1 < chunks))
        def _():
            enter(tick // leaf_count + 1)

    @pl.loop(0, units)
    def _(unit):
        for stage in range(len(stages)):
            exchange(stage, unit).wait_send()
        write_out(unit).wait()

    @pl.loop(0, leaf_count)
    def _(leaf):
        write_placed(leaf).wait()


def output_kernel(placed, skeleton, out, placed_v, skeleton_v, out_v, placed_sem, skeleton_sem, out_sem):
    leaf_count, _, leaf_rows, _ = placed_v.shape

    def loads(leaf):
        return (
            pltpu.make_async_copy(placed.at[leaf], placed_v.at[leaf], placed_sem.at[leaf]),
            pltpu.make_async_copy(skeleton.at[leaf], skeleton_v.at[leaf], skeleton_sem.at[leaf]),
        )

    def store(leaf):
        return pltpu.make_async_copy(out_v.at[leaf], out.at[pl.ds(leaf * leaf_rows, leaf_rows), :], out_sem.at[leaf])

    for leaf in range(leaf_count):
        for copy in loads(leaf):
            copy.start()
    for leaf in range(leaf_count):
        for copy in loads(leaf):
            copy.wait()
        out_v[leaf] = dot3((placed_v[leaf, 0], placed_v[leaf, 1]), (skeleton_v[leaf, 0], skeleton_v[leaf, 1]))
        store(leaf).start()
    for leaf in range(leaf_count):
        store(leaf).wait()


def on_device(rhs_grid, leaf_order, source_basis, transfer, target_basis):
    leaf_count, leaf_rows = leaf_order.shape
    points, columns = rhs_grid.shape
    rank = source_basis.shape[2]
    levels = transfer.shape[0]
    low_bits = leaf_count.bit_length() - 1
    row_bits = lax.axis_size("row").bit_length() - 1
    col_bits = lax.axis_size("col").bit_length() - 1
    stages = [("row", bit) for bit in range(row_bits)] + [("col", bit) for bit in range(col_bits)]
    count = len(stages)
    offsets = [0]
    for axis, bit in stages[1:]:
        if axis == "col":
            offsets.append(offsets[-1] + 1)
        else:
            offsets.append(offsets[-1] + (FAR if bit == row_bits - 1 else MIDDLE))
    chunks = columns // WIDTH
    units = leaf_count * chunks
    hbm = pl.BlockSpec(memory_space=pl.ANY)
    skeleton, placed = pl.pallas_call(
        functools.partial(kernel, stages, offsets, low_bits),
        out_shape=[
            jax.ShapeDtypeStruct((leaf_count, 2, rank, columns), BF16),
            jax.ShapeDtypeStruct((leaf_count, 2, leaf_rows, rank), BF16),
        ],
        in_specs=[hbm, pl.BlockSpec(memory_space=pltpu.VMEM), hbm, hbm, hbm],
        out_specs=[hbm, hbm],
        scratch_shapes=[
            pltpu.VMEM((chunks, points, WIDTH), F32),
            pltpu.VMEM((leaf_count, rank, leaf_rows), F32),
            pltpu.VMEM((leaf_count, rank, leaf_rows), F32),
            pltpu.VMEM(transfer.shape, F32),
            pltpu.VMEM((leaf_count, rank, leaf_rows), BF16),
            pltpu.VMEM((leaf_count, rank, leaf_rows), BF16),
            pltpu.VMEM((leaf_count, 2, leaf_rows, rank), BF16),
            pltpu.VMEM((count, units, rank, WIDTH), F32),
            pltpu.VMEM((count, units, rank, WIDTH), F32),
            pltpu.VMEM((units, 2, rank, WIDTH), BF16),
            pltpu.SemaphoreType.DMA((chunks,)),
            pltpu.SemaphoreType.DMA((leaf_count + 1,)),
            pltpu.SemaphoreType.DMA((levels,)),
            pltpu.SemaphoreType.DMA((count, units)),
            pltpu.SemaphoreType.DMA((count, units)),
            pltpu.SemaphoreType.DMA((units,)),
            pltpu.SemaphoreType.DMA((leaf_count,)),
        ],
        compiler_params=pltpu.CompilerParams(
            collective_id=0, has_side_effects=True, vmem_limit_bytes=56 * 2**20
        ),
    )(rhs_grid, leaf_order, source_basis.swapaxes(1, 2), transfer, target_basis.swapaxes(1, 2))
    return pl.pallas_call(
        output_kernel,
        out_shape=jax.ShapeDtypeStruct((points, columns), F32),
        in_specs=[hbm, hbm],
        out_specs=hbm,
        scratch_shapes=[
            pltpu.VMEM(placed.shape, BF16),
            pltpu.VMEM(skeleton.shape, BF16),
            pltpu.VMEM((leaf_count, leaf_rows, columns), F32),
            pltpu.SemaphoreType.DMA((leaf_count,)),
            pltpu.SemaphoreType.DMA((leaf_count,)),
            pltpu.SemaphoreType.DMA((leaf_count,)),
        ],
        compiler_params=pltpu.CompilerParams(vmem_limit_bytes=56 * 2**20),
    )(placed, skeleton)


def solution(mesh):
    in_specs = (
        P(("row", "col"), None),
        P(("row", "col"), None),
        P(("row", "col"), None, None),
        P(None, ("row", "col"), None, None),
        P(("row", "col"), None, None),
    )
    out_specs = P(("row", "col"), None)
    return jax.shard_map(
        on_device, mesh=mesh, in_specs=in_specs, out_specs=out_specs, check_vma=False
    )
```
